32 devices in a mesh: ves: 4 (over x, core), shard: 8 (over z, y).
Axes of the slice: x: 2, y: 2, z: 4, core: 2. Of those that a mesh axis runs over, the one named last changes fastest.
Arguments:
- displacement: float32 [3, 8, 256, 128], P(None, 'ves', 'shard'), may hold values from -6 to 6
- tension: float32 [8], P('ves'), may hold values from 2 to 8
- bending: float32 [8], P('ves'), may hold values from 0.2 to 0.8
- offset: float32 [3, 8, 256, 128], P(None, 'ves', 'shard'), may hold values from 0 to 1
- owner: int32 [8, 256, 128], P('ves', 'shard'), may hold values from 0 to 31, as said below
- cell: int32 [8, 256, 128], P('ves', 'shard'), may hold values from 0 to 131071
- populations: float32 [64, 19, 256, 256], P(('ves', 'shard')), may hold values from 0 to 1, as said below
Outputs:
- membrane_force: float32 [3, 8, 256, 128], P(None, 'ves', 'shard')
- force_field: float32 [64, 3, 256, 256], P(('ves', 'shard'))
- new_populations: float32 [64, 19, 256, 256], P(('ves', 'shard'))
The draws below stay inside these ranges and needn't reach their ends.
Inputs may be any that keep to these rules, and one draw needn't show every extreme that they name: The points of one device name any one owner at most 512 times, and some owner is named exactly 512 times by the points of every device. `populations`: entries are positive.
All inputs are finite; a program needn't handle non-finite values.
Results may differ from the reference program's by a relative error of at most 0.0061.
Values sent between devices are 32-bit elements; how exact they have to be, the bound alone decides.
A program may use at most 128 MiB of HBM per device.

```python
import math
import jax
import jax.numpy as jnp
from jax import lax

NXY = 256
SLAB = 2
LAT = 256
LON = 128
VES_GRP = 2
NVES = 8
NZ = 64
N_VES = 4
N_SHARD = 8


lattice_weights = [1.0 / 18, 1.0 / 36, 1.0 / 36, 1.0 / 36, 1.0 / 36, 1.0 / 18, 1.0 / 36, 1.0 / 36, 1.0 / 36, 1.0 / 36, 1.0 / 3, 1.0 / 18, 1.0 / 18, 1.0 / 18, 1.0 / 18, 1.0 / 36, 1.0 / 36, 1.0 / 36, 1.0 / 36]


def draw_populations(key, part):
    shape = (NZ, 19, NXY, NXY)
    table = jnp.array(lattice_weights, jnp.float32).reshape(1, 19, 1, 1)
    level = jax.random.uniform(key, shape, jnp.float32, 0.5, 1.5)
    return (level * table).astype(jnp.float32)


def draw_owner(key, part):
    device_count = N_VES * N_SHARD
    row_count = LAT // N_SHARD
    point_count = VES_GRP * row_count * LON
    capacity = 2 * point_count // device_count
    slot_count = device_count * capacity
    hottest = jax.random.randint(jax.random.fold_in(key, 1), (), 0, device_count)
    extra_load = jax.random.randint(jax.random.fold_in(key, 2), (device_count,), 0, 4) * 1024
    extra_load = jnp.where(jnp.arange(device_count) == hottest, 8192, extra_load)
    slot_dest = jnp.arange(slot_count, dtype=jnp.int32) // capacity

    def one_block(block_number):
        jitter = jax.random.randint(jax.random.fold_in(jax.random.fold_in(key, 3), block_number), (slot_count,), 0, 4096)
        ranking = (jitter + extra_load[slot_dest]) * slot_count + jnp.arange(slot_count, dtype=jnp.int32)
        picked_slots = jax.lax.top_k(ranking, point_count)[1]
        chosen = slot_dest[picked_slots]
        mixer = jax.random.permutation(jax.random.fold_in(jax.random.fold_in(key, 4), block_number), point_count)
        return chosen[mixer]
    blocks = jax.vmap(one_block)(jnp.arange(device_count))
    blocks = blocks.reshape(N_VES, N_SHARD, VES_GRP, row_count, LON)
    return blocks.transpose(0, 2, 1, 3, 4).reshape(N_VES * VES_GRP, LAT, LON).astype(jnp.int32)


def set_ends(entries, key, smallest, high):
    spot = [jax.random.randint(jax.random.fold_in(key, axis), (), 0, length) for axis, length in enumerate(entries.shape)]
    widest = entries.shape.index(max(entries.shape))
    beside = spot[:widest] + [(spot[widest] + 1) % entries.shape[widest]] + spot[widest + 1:]
    return entries.at[tuple(spot)].set(smallest).at[tuple(beside)].set(high)


def levels(key, extent, split, smallest, high):
    level = 1.0
    for dim, parts in split:
        draws = jax.random.uniform(jax.random.fold_in(jax.random.fold_in(key, 6), dim), (parts,), jnp.float32, smallest / len(split), high / len(split))
        level = level * jnp.repeat(jnp.exp(draws), extent[dim] // parts).reshape((-1,) + (1,) * (len(extent) - 1 - dim))
    return level


def scatter_about(stream_key, dims, deviation, limit, split=(), held_as=jnp.bfloat16):
    values = deviation * jax.random.normal(stream_key, dims, jnp.float32)
    if split:
        values = values * levels(stream_key, dims, split, -0.22, 0.18)
    return jnp.clip(values, -limit, limit).astype(held_as)


def setup_inputs(seed: int = 0) -> dict:
    seeds = jax.random.split(jax.random.key(seed), 8)
    displacement = scatter_about(seeds[0], (3, NVES, LAT, LON), 1.0, 6.0, ((1, 4), (2, 8)), jnp.float32)
    tension = jnp.clip(jnp.exp(math.log(8.0) - 1.3862944 * jax.random.uniform(seeds[1], (NVES,), jnp.float32) ** levels(seeds[1], (NVES,), ((0, 4),), -0.2, 0.2)), 2.0, 8.0)
    bending = jnp.clip(jnp.exp(math.log(0.8) - 1.3862944 * jax.random.uniform(seeds[2], (NVES,), jnp.float32) ** levels(seeds[2], (NVES,), ((0, 4),), -0.2, 0.2)), 0.2, 0.8)
    offset = jnp.clip(1.0 * jax.random.uniform(seeds[3], (3, NVES, LAT, LON), jnp.float32) ** levels(seeds[3], (3, NVES, LAT, LON), ((1, 4), (2, 8)), -0.2, 0.2), 0.0, 1.0)
    owner = draw_owner(jax.random.fold_in(seeds[7], 71), 0)
    cell = set_ends(jax.random.randint(seeds[5], (NVES, LAT, LON), 0, SLAB * NXY * NXY), jax.random.fold_in(seeds[5], 1), 0, (SLAB * NXY * NXY) - 1).astype(jnp.int32)
    populations = draw_populations(jax.random.fold_in(seeds[7], 71), 0)
    return {"displacement": displacement, "tension": tension, "bending": bending, "offset": offset, "owner": owner, "cell": cell, "populations": populations}


relax_time = 0.8
velocity_x = [0, 1, -1, 0, 0, 0, 1, -1, 0, 0, 0, 1, -1, 0, 0, 1, 1, -1, -1]
velocity_y = [0, 0, 0, 1, -1, 0, 0, 0, 1, -1, 0, 0, 0, 1, -1, 1, -1, 1, -1]
velocity_z = [1, 1, 1, 1, 1, -1, -1, -1, -1, -1, 0, 0, 0, 0, 0, 0, 0, 0, 0]
lattice_weights = [1.0 / 18, 1.0 / 36, 1.0 / 36, 1.0 / 36, 1.0 / 36, 1.0 / 18, 1.0 / 36, 1.0 / 36, 1.0 / 36, 1.0 / 36, 1.0 / 3, 1.0 / 18, 1.0 / 18, 1.0 / 18, 1.0 / 18, 1.0 / 36, 1.0 / 36, 1.0 / 36, 1.0 / 36]


def kernel_weight(distance):
    return 0.25 * (1.0 + jnp.cos(0.5 * math.pi * distance))


def surface_laplacian(field):
    padded = jnp.pad(field, ((0, 0), (0, 0), (1, 1), (0, 0)))
    center = padded[:, :, 1:-1]
    return padded[:, :, 2:] + padded[:, :, :-2] + jnp.roll(center, 1, 3) + jnp.roll(center, -1, 3) - 4.0 * center


def reference(displacement, tension, bending, offset, owner, cell, populations):
    first = surface_laplacian(displacement)
    second = surface_laplacian(first)
    membrane_force = tension[None, :, None, None] * first - bending[None, :, None, None] * second
    forces = membrane_force.reshape(3, -1)
    fraction = offset.reshape(3, -1)
    owner_flat = owner.reshape(-1).astype(jnp.int32)
    cell_flat = cell.reshape(-1).astype(jnp.int32)
    plane = cell_flat // (NXY * NXY)
    column_x = (cell_flat // NXY) % NXY
    column_y = cell_flat % NXY
    base_z = owner_flat * SLAB + plane
    coords = jnp.arange(3, dtype=jnp.int32)
    field = jnp.zeros((NZ, 3, NXY, NXY), jnp.float32)
    for reach_z in range(-1, 3):
        scaled = forces * kernel_weight(fraction[2] - reach_z)[None, :]
        plane_z = (base_z + reach_z) % NZ
        for reach_x in range(-1, 3):
            left = (scaled * kernel_weight(fraction[0] - reach_x)[None, :]).astype(jnp.bfloat16)
            left = lax.optimization_barrier(left).astype(jnp.float32)
            place_x = (column_x + reach_x) % NXY
            for reach_y in range(-1, 3):
                right = kernel_weight(fraction[1] - reach_y).astype(jnp.bfloat16)
                right = lax.optimization_barrier(right).astype(jnp.float32)
                place_y = (column_y + reach_y) % NXY
                term = left * right[None, :]
                field = field.at[plane_z[:, None], coords[None, :], place_x[:, None], place_y[:, None]].add(term.T)
    density = jnp.sum(populations, 1)
    moment_x = jnp.zeros_like(density)
    moment_y = jnp.zeros_like(density)
    moment_z = jnp.zeros_like(density)
    for item in range(19):
        moment_x = moment_x + velocity_x[item] * populations[:, item]
        moment_y = moment_y + velocity_y[item] * populations[:, item]
        moment_z = moment_z + velocity_z[item] * populations[:, item]
    flow_x = (moment_x + 0.5 * field[:, 0]) / density
    flow_y = (moment_y + 0.5 * field[:, 1]) / density
    flow_z = (moment_z + 0.5 * field[:, 2]) / density
    speed_sq = flow_x * flow_x + flow_y * flow_y + flow_z * flow_z
    moved = []
    for item in range(19):
        ex, ey, ez = velocity_x[item], velocity_y[item], velocity_z[item]
        weight = lattice_weights[item]
        along = ex * flow_x + ey * flow_y + ez * flow_z
        equilibrium = weight * density * (1.0 + 3.0 * along + 4.5 * along * along - 1.5 * speed_sq)
        push = (ex - flow_x) * field[:, 0] + (ey - flow_y) * field[:, 1] + (ez - flow_z) * field[:, 2]
        facing = ex * field[:, 0] + ey * field[:, 1] + ez * field[:, 2]
        source = weight * (3.0 * push + 9.0 * along * facing)
        current = populations[:, item]
        post = current - (current - equilibrium) / relax_time + (1.0 - 0.5 / relax_time) * source
        moved.append(jnp.roll(post, (ez, ex, ey), (0, 1, 2)))
    return membrane_force, field, jnp.stack(moved, 1)
```

```python
import math

import jax
import jax.numpy as jnp
from jax import lax
from jax.experimental import pallas as pl
from jax.experimental.pallas import tpu as pltpu
from jax.sharding import PartitionSpec as P

relax_time = 0.8
velocity_x = [0, 1, -1, 0, 0, 0, 1, -1, 0, 0, 0, 1, -1, 0, 0, 1, 1, -1, -1]
velocity_y = [0, 0, 0, 1, -1, 0, 0, 0, 1, -1, 0, 0, 0, 1, -1, 1, -1, 1, -1]
velocity_z = [1, 1, 1, 1, 1, -1, -1, -1, -1, -1, 0, 0, 0, 0, 0, 0, 0, 0, 0]
lattice_weights = [
    1.0 / 18,
    1.0 / 36,
    1.0 / 36,
    1.0 / 36,
    1.0 / 36,
    1.0 / 18,
    1.0 / 36,
    1.0 / 36,
    1.0 / 36,
    1.0 / 36,
    1.0 / 3,
    1.0 / 18,
    1.0 / 18,
    1.0 / 18,
    1.0 / 18,
    1.0 / 36,
    1.0 / 36,
    1.0 / 36,
    1.0 / 36,
]


def passed_along(value, axis, steps):
    count = lax.axis_size(axis)
    pairs = [(source, (source + steps) % count) for source in range(count)]
    return lax.ppermute(value, axis, pairs)


def with_halo(x, axis, dim, width):
    devices, length = (lax.axis_size(axis), x.shape[dim])
    up = [(i, i + 1) for i in range(devices - 1)]
    down = [(j, i) for i, j in up]
    last = lax.slice_in_dim(x, length - width, length, axis=dim)
    initial = lax.slice_in_dim(x, 0, width, axis=dim)
    before = lax.ppermute(last, axis, up)
    after = lax.ppermute(initial, axis, down)
    return jnp.concatenate([before, x, after], axis=dim)


def laplacian(padded):
    center = padded[:, :, 1:-1]
    return (
        padded[:, :, 2:]
        + padded[:, :, :-2]
        + jnp.roll(center, 1, 3)
        + jnp.roll(center, -1, 3)
        - 4.0 * center
    )


def membrane(displacement, tension, bending):
    padded = with_halo(displacement, "shard", 2, 2)
    wide_first = laplacian(padded)
    rows = wide_first.shape[2]
    place = lax.broadcasted_iota(jnp.int32, (1, 1, rows, 1), 2)
    index = lax.axis_index("shard")
    outside = ((place == 0) & (index == 0)) | (
        (place == rows - 1) & (index == lax.axis_size("shard") - 1)
    )
    wide_first = jnp.where(outside, 0.0, wide_first)
    second = laplacian(wide_first)
    first = wide_first[:, :, 1:-1]
    return tension[None, :, None, None] * first - bending[None, :, None, None] * second


WINDOW = 16
ROWS = 24
BLOCK = 256


def weights(fraction):
    angle = (0.5 * math.pi) * fraction
    c, s = jnp.cos(angle), jnp.sin(angle)
    return [0.25 * (1.0 - s), 0.25 * (1.0 + c), 0.25 * (1.0 + s), 0.25 * (1.0 - c)]


def prepared(listed, slab, width):
    key = listed[6].astype(jnp.int32)
    windows = width // WINDOW
    bounds = jnp.arange(windows + 1, dtype=jnp.int32) * (WINDOW * slab * width)
    starts = jnp.sum((key[None, :] < bounds[:, None]).astype(jnp.int32), 1)
    x = key // (slab * width)
    plane = key // width % slab
    y = key % width
    values = jnp.stack(
        [listed[0], listed[1], listed[2]]
        + weights(listed[3])
        + weights(listed[4])
        + weights(listed[5])
        + [jnp.zeros_like(listed[0])],
        0,
    )
    places = jnp.stack([x, plane, y] + [jnp.zeros_like(x)] * 5, 0)
    return starts, values, places


def spread_list(starts, values_ref, places_ref, acc, shift, planes, width):
    windows = width // WINDOW
    row_id = lax.broadcasted_iota(jnp.int32, (ROWS, BLOCK), 0)
    y_id = lax.broadcasted_iota(jnp.int32, (width, BLOCK), 0)

    def pick(rel, parts):
        result = jnp.zeros(rel.shape, jnp.float32)
        for k in range(4):
            result = jnp.where(rel == k, parts[k], result)
        return result

    @pl.loop(0, windows)
    def _(w):
        begin = starts[w] // BLOCK
        end = (starts[w + 1] + (BLOCK - 1)) // BLOCK
        base = w * WINDOW

        @pl.loop(begin, end)
        def _(b):
            at = pl.ds(pl.multiple_of(b * BLOCK, BLOCK), BLOCK)

            def value(r):
                return values_ref[r : r + 1, at]

            x = places_ref[0:1, at] - base
            x = jnp.where((x >= 0) & (x < WINDOW), x, 4 * ROWS)
            plane = places_ref[1:2, at]
            y = places_ref[2:3, at]
            weight_x = pick(row_id - x, [value(3 + k) for k in range(4)])
            right = pick(
                (y_id - y + 1) & (width - 1), [value(7 + k) for k in range(4)]
            ).astype(jnp.bfloat16)
            lefts = []
            for q in planes:
                weight_z = pick(q + 1 + shift - plane, [value(11 + k) for k in range(4)])
                for c in range(3):
                    lefts.append((value(c) * weight_z) * weight_x)
            left = jnp.concatenate(lefts, 0).astype(jnp.bfloat16)
            product = lax.dot_general(
                left, right, (((1,), (1,)), ((), ())), preferred_element_type=jnp.float32
            )
            rows = pl.ds(pl.multiple_of(base, 8), ROWS)
            for n, q in enumerate(planes):
                for c in range(3):
                    i = n * 3 + c
                    acc[q * 3 + c, rows, :] += product[i * ROWS : (i + 1) * ROWS]


def spread_own(own, slab, width):
    starts, values, places = own

    def kernel(starts_ref, values_ref, places_ref, acc):
        acc[...] = jnp.zeros_like(acc)
        spread_list(starts_ref, values_ref, places_ref, acc, 0, range(slab), width)

    vmem = pl.BlockSpec(memory_space=pltpu.VMEM)
    return pl.pallas_call(
        kernel,
        out_shape=jax.ShapeDtypeStruct((slab * 3, width + ROWS - WINDOW, width), jnp.float32),
        in_specs=[pl.BlockSpec(memory_space=pltpu.SMEM), vmem, vmem],
        out_specs=vmem,
        name="spread_own",
        cost_estimate=pl.CostEstimate(
            flops=20_000_000_000, bytes_accessed=4_000_000, transcendentals=0
        ),
    )(starts, values, places)


def spread_others(total, below, above, slab, width):
    def kernel(s0, v0, p0, s1, v1, p1, total_ref, out, acc):
        acc[...] = total_ref[...]
        spread_list(s0, v0, p0, acc, slab, (0, 1), width)
        spread_list(s1, v1, p1, acc, -slab, (slab - 1,), width)
        for i in range(slab * 3):
            out[i] = acc[i, 1 : width + 1, :]
            out[i, width - 1 : width, :] += acc[i, 0:1, :]
            out[i, 0:2, :] += acc[i, width + 1 : width + 3, :]

    vmem = pl.BlockSpec(memory_space=pltpu.VMEM)
    smem = pl.BlockSpec(memory_space=pltpu.SMEM)
    return pl.pallas_call(
        kernel,
        out_shape=jax.ShapeDtypeStruct((slab * 3, width, width), jnp.float32),
        in_specs=[smem, vmem, vmem, smem, vmem, vmem, vmem],
        out_specs=vmem,
        scratch_shapes=[pltpu.VMEM(total.shape, jnp.float32)],
        name="spread_others",
        cost_estimate=pl.CostEstimate(
            flops=20_000_000_000, bytes_accessed=6_000_000, transcendentals=0
        ),
    )(*below, *above, total)


def dispatched(membrane_force, offset, owner, cell, device_count, cells):
    point_count = owner.size
    capacity = 2 * point_count // device_count
    slot_total = device_count * capacity
    owner = owner.reshape(point_count)
    cell = cell.reshape(point_count)
    devices = jnp.arange(device_count, dtype=jnp.int32)
    counts = jnp.sum((owner[None, :] == devices[:, None]).astype(jnp.int32), 1)
    filler_ends = jnp.cumsum(capacity - counts)
    filler = jnp.arange(slot_total - point_count, dtype=jnp.int32)
    filler_owner = jnp.sum((filler[None, :] >= filler_ends[:, None]).astype(jnp.int32), 0)
    span = 2 * cells
    key = jnp.concatenate([owner * span + cell, filler_owner * span + cells])
    payload = jnp.concatenate(
        [membrane_force.reshape(3, point_count), offset.reshape(3, point_count)], 0
    )
    payload = jnp.pad(payload, ((0, 0), (0, slot_total - point_count)))
    ordered = lax.sort(
        (key,) + tuple(payload[i] for i in range(6)), num_keys=1, is_stable=False
    )
    tag = (ordered[0] % span).astype(jnp.float32)
    send = jnp.stack(
        [v.reshape(device_count, capacity) for v in list(ordered[1:]) + [tag]], 1
    )
    got = lax.all_to_all(send, ("ves", "shard"), split_axis=0, concat_axis=0, tiled=True)
    return got.transpose(1, 0, 2).reshape(7, slot_total)


def collide(populations, field):
    density = jnp.sum(populations, 1)
    moment_x = jnp.zeros_like(density)
    moment_y = jnp.zeros_like(density)
    moment_z = jnp.zeros_like(density)
    for item in range(19):
        moment_x = moment_x + velocity_x[item] * populations[:, item]
        moment_y = moment_y + velocity_y[item] * populations[:, item]
        moment_z = moment_z + velocity_z[item] * populations[:, item]
    flow_x = (moment_x + 0.5 * field[:, 0]) / density
    flow_y = (moment_y + 0.5 * field[:, 1]) / density
    flow_z = (moment_z + 0.5 * field[:, 2]) / density
    speed_sq = flow_x * flow_x + flow_y * flow_y + flow_z * flow_z
    result = []
    for item in range(19):
        ex, ey, ez = (velocity_x[item], velocity_y[item], velocity_z[item])
        weight = lattice_weights[item]
        along = ex * flow_x + ey * flow_y + ez * flow_z
        equilibrium = weight * density * (1.0 + 3.0 * along + 4.5 * along * along - 1.5 * speed_sq)
        push = (
            (ex - flow_x) * field[:, 0] + (ey - flow_y) * field[:, 1] + (ez - flow_z) * field[:, 2]
        )
        facing = ex * field[:, 0] + ey * field[:, 1] + ez * field[:, 2]
        source = weight * (3.0 * push + 9.0 * along * facing)
        current = populations[:, item]
        result.append(
            current - (current - equilibrium) / relax_time + (1.0 - 0.5 / relax_time) * source
        )
    return jnp.stack(result, 1)


def on_device(displacement, tension, bending, offset, owner, cell, populations):
    membrane_force = membrane(displacement, tension, bending)
    device_count = lax.axis_size("ves") * lax.axis_size("shard")
    slab, width = (populations.shape[0], populations.shape[2])
    cells = slab * width * width
    got = dispatched(membrane_force, offset, owner, cell, device_count, cells)
    tag = got[6].astype(jnp.int32)
    plane, x, y = (tag // (width * width), tag // width % width, tag % width)
    key = jnp.where(tag >= cells, cells, (x * slab + plane) * width + y)
    ordered = lax.sort(
        (key,) + tuple(got[i] for i in range(6)), num_keys=1, is_stable=False
    )
    listed = jnp.stack(list(ordered[1:]) + [ordered[0].astype(jnp.float32)], 0)
    below = passed_along(listed, ("ves", "shard"), 1)
    above = passed_along(listed, ("ves", "shard"), -1)
    total = spread_own(prepared(listed, slab, width), slab, width)
    force_field = spread_others(
        total, prepared(below, slab, width), prepared(above, slab, width), slab, width
    ).reshape(slab, 3, width, width)
    post = collide(populations, force_field)
    low_part = passed_along(post[slab - 1, 0:5], ("ves", "shard"), 1)
    high_part = passed_along(post[0, 5:10], ("ves", "shard"), -1)
    low_source = jnp.concatenate([low_part[None], post[: slab - 1, 0:5]], 0)
    high_source = jnp.concatenate([post[1:, 5:10], high_part[None]], 0)
    source = jnp.concatenate([low_source, high_source, post[:, 10:]], 1)
    moved = [
        jnp.roll(source[:, item], (velocity_x[item], velocity_y[item]), (1, 2))
        for item in range(19)
    ]
    return (membrane_force, force_field, jnp.stack(moved, 1))


def solution(mesh):
    return jax.shard_map(
        on_device,
        mesh=mesh,
        in_specs=(
            P(None, "ves", "shard", None),
            P("ves"),
            P("ves"),
            P(None, "ves", "shard", None),
            P("ves", "shard", None),
            P("ves", "shard", None),
            P(("ves", "shard"), None, None, None),
        ),
        out_specs=(
            P(None, "ves", "shard", None),
            P(("ves", "shard"), None, None, None),
            P(("ves", "shard"), None, None, None),
        ),
        check_vma=False,
    )
```

```python
import math

import jax
import jax.numpy as jnp
from jax import lax
from jax.experimental import pallas as pl
from jax.experimental.pallas import tpu as pltpu
from jax.sharding import PartitionSpec as P


relax_time = 0.8
velocity_x = [0, 1, -1, 0, 0, 0, 1, -1, 0, 0, 0, 1, -1, 0, 0, 1, 1, -1, -1]
velocity_y = [0, 0, 0, 1, -1, 0, 0, 0, 1, -1, 0, 0, 0, 1, -1, 1, -1, 1, -1]
velocity_z = [1, 1, 1, 1, 1, -1, -1, -1, -1, -1, 0, 0, 0, 0, 0, 0, 0, 0, 0]
lattice_weights = [
    1.0 / 18,
    1.0 / 36,
    1.0 / 36,
    1.0 / 36,
    1.0 / 36,
    1.0 / 18,
    1.0 / 36,
    1.0 / 36,
    1.0 / 36,
    1.0 / 36,
    1.0 / 3,
    1.0 / 18,
    1.0 / 18,
    1.0 / 18,
    1.0 / 18,
    1.0 / 36,
    1.0 / 36,
    1.0 / 36,
    1.0 / 36,
]


def passed_along(value, axis, steps):
    count = lax.axis_size(axis)
    pairs = [(source, (source + steps) % count) for source in range(count)]
    return lax.ppermute(value, axis, pairs)


def with_halo(x, axis, dim, width):
    devices, length = (lax.axis_size(axis), x.shape[dim])
    up = [(i, i + 1) for i in range(devices - 1)]
    down = [(j, i) for i, j in up]
    last = lax.slice_in_dim(x, length - width, length, axis=dim)
    initial = lax.slice_in_dim(x, 0, width, axis=dim)
    before = lax.ppermute(last, axis, up)
    after = lax.ppermute(initial, axis, down)
    return jnp.concatenate([before, x, after], axis=dim)


def laplacian(padded):
    center = padded[:, :, 1:-1]
    return (
        padded[:, :, 2:]
        + padded[:, :, :-2]
        + jnp.roll(center, 1, 3)
        + jnp.roll(center, -1, 3)
        - 4.0 * center
    )


def membrane(displacement, tension, bending):
    padded = with_halo(displacement, "shard", 2, 2)
    wide_first = laplacian(padded)
    rows = wide_first.shape[2]
    place = lax.broadcasted_iota(jnp.int32, (1, 1, rows, 1), 2)
    index = lax.axis_index("shard")
    outside = ((place == 0) & (index == 0)) | (
        (place == rows - 1) & (index == lax.axis_size("shard") - 1)
    )
    wide_first = jnp.where(outside, 0.0, wide_first)
    second = laplacian(wide_first)
    first = wide_first[:, :, 1:-1]
    return tension[None, :, None, None] * first - bending[None, :, None, None] * second


WINDOW = 16
ROWS = 24
BLOCK = 256


HALF_PI = 0.5 * math.pi
COSINE = [(-1.0) ** n * HALF_PI ** (2 * n) / math.factorial(2 * n) for n in range(8)]
SINE = [(-1.0) ** n * HALF_PI ** (2 * n + 1) / math.factorial(2 * n + 1) for n in range(8)]


def weights(fraction):
    square = fraction * fraction
    c = jnp.full_like(square, COSINE[-1])
    s = jnp.full_like(square, SINE[-1])
    for n in range(6, -1, -1):
        c = c * square + COSINE[n]
        s = s * square + SINE[n]
    s = s * fraction
    return [0.25 * (1.0 - s), 0.25 * (1.0 + c), 0.25 * (1.0 + s), 0.25 * (1.0 - c)]


def bits(count):
    return (count - 1).bit_length()


def spread_list(starts, list_ref, acc, shift, planes, slab, ranges):
    width = acc.shape[2]
    row_id = lax.broadcasted_iota(jnp.int32, (ROWS, BLOCK), 0)
    y_id = lax.broadcasted_iota(jnp.int32, (width, BLOCK), 0)

    def pick(rel, parts):
        result = jnp.zeros(rel.shape, jnp.float32)
        for k in range(4):
            result = jnp.where(rel == k, parts[k], result)
        return result

    def window(w):
        begin = starts[w] // BLOCK
        end = (starts[w + 1] + (BLOCK - 1)) // BLOCK
        base = w * WINDOW

        @pl.loop(begin, end)
        def _(b):
            at = pl.ds(pl.multiple_of(b * BLOCK, BLOCK), BLOCK)
            phi = weights(list_ref[3:6, at])
            key = list_ref[6:7, at].astype(jnp.int32)
            y = key & ((1 << bits(width)) - 1)
            plane = (key >> bits(width)) & ((1 << bits(slab)) - 1)
            x = (key >> (bits(width) + bits(slab))) - base
            x = jnp.where((x >= 0) & (x < WINDOW), x, 4 * ROWS)
            weight_x = pick(row_id - x, [phi[k][0:1] for k in range(4)])
            right = pick((y_id - (y - 1)) & (width - 1), [phi[k][1:2] for k in range(4)])
            lefts = []
            for q in planes:
                weight_z = pick(q + 1 + shift - plane, [phi[k][2:3] for k in range(4)])
                for c in range(3):
                    lefts.append((list_ref[c : c + 1, at] * weight_z) * weight_x)
            product = lax.dot_general(
                jnp.concatenate(lefts, 0).astype(jnp.bfloat16),
                right.astype(jnp.bfloat16),
                (((1,), (1,)), ((), ())),
                preferred_element_type=jnp.float32,
            )
            rows = pl.ds(pl.multiple_of(base, 8), ROWS)
            for n, q in enumerate(planes):
                for c in range(3):
                    i = n * 3 + c
                    acc[q * 3 + c, rows, :] += product[i * ROWS : (i + 1) * ROWS]

    for first, last in ranges:

        @pl.loop(first, last)
        def _(w):
            window(w)


VMEM = pl.BlockSpec(memory_space=pltpu.VMEM)
SMEM = pl.BlockSpec(memory_space=pltpu.SMEM)


def cost(flops):
    return pl.CostEstimate(flops=flops, bytes_accessed=4_000_000, transcendentals=0)


def starts_of(listed, windows):
    return listed[7, : windows + 1].astype(jnp.int32)


def spread_own(listed, slab, width):
    windows = width // WINDOW

    def kernel(starts, list_ref, acc):
        acc[...] = jnp.zeros_like(acc)
        spread_list(starts, list_ref, acc, 0, range(slab), slab, [(0, windows)])

    return pl.pallas_call(
        kernel,
        out_shape=jax.ShapeDtypeStruct((slab * 3, width + ROWS - WINDOW, width), jnp.float32),
        in_specs=[SMEM, VMEM],
        out_specs=VMEM,
        name="spread_own",
        cost_estimate=cost(20_000_000_000),
    )(starts_of(listed, windows), listed)


def spread_rest(total, below, above, slab, ranges, rows):
    width = total.shape[2]
    windows = width // WINDOW

    def kernel(s0, l0, s1, l1, total_ref, acc, out):
        acc[...] = total_ref[...]
        spread_list(s0, l0, acc, slab, (0, 1), slab, ranges)
        spread_list(s1, l1, acc, -slab, (slab - 1,), slab, ranges)
        for i in range(slab * 3):
            out[i] = acc[i, 1 : rows + 1, :]
            out[i, 0:2, :] += acc[i, width + 1 : width + 3, :]
            if rows == width:
                out[i, width - 1 : width, :] += acc[i, 0:1, :]

    return pl.pallas_call(
        kernel,
        out_shape=(
            jax.ShapeDtypeStruct(total.shape, jnp.float32),
            jax.ShapeDtypeStruct((slab * 3, rows, width), jnp.float32),
        ),
        in_specs=[SMEM, VMEM, SMEM, VMEM, VMEM],
        out_specs=(VMEM, VMEM),
        name="spread_rest",
        cost_estimate=cost(15_000_000_000),
    )(starts_of(below, windows), below, starts_of(above, windows), above, total)


def dispatched(membrane_force, offset, owner, cell, device_count, cells):
    point_count = owner.size
    capacity = 2 * point_count // device_count
    slot_total = device_count * capacity
    owner = owner.reshape(point_count)
    cell = cell.reshape(point_count)
    devices = jnp.arange(device_count, dtype=jnp.int32)
    counts = jnp.sum((owner[None, :] == devices[:, None]).astype(jnp.int32), 1)
    filler_ends = jnp.cumsum(capacity - counts)
    filler = jnp.arange(slot_total - point_count, dtype=jnp.int32)
    filler_owner = jnp.sum((filler[None, :] >= filler_ends[:, None]).astype(jnp.int32), 0)
    span = 2 * cells
    key = jnp.concatenate([owner * span + cell, filler_owner * span + cells])
    payload = jnp.concatenate(
        [membrane_force.reshape(3, point_count), offset.reshape(3, point_count)], 0
    )
    payload = jnp.pad(payload, ((0, 0), (0, slot_total - point_count)))
    ordered = lax.sort(
        (key,) + tuple(payload[i] for i in range(6)), num_keys=1, is_stable=False
    )
    tag = (ordered[0] % span).astype(jnp.float32)
    send = jnp.stack(
        [v.reshape(device_count, capacity) for v in list(ordered[1:]) + [tag]], 1
    )
    got = lax.all_to_all(send, ("ves", "shard"), split_axis=0, concat_axis=0, tiled=True)
    return got.transpose(1, 0, 2).reshape(7, slot_total)


def collide(populations, field, items):
    density = jnp.sum(populations, 0)
    moment_x = jnp.zeros_like(density)
    moment_y = jnp.zeros_like(density)
    moment_z = jnp.zeros_like(density)
    for item in range(19):
        moment_x = moment_x + velocity_x[item] * populations[item]
        moment_y = moment_y + velocity_y[item] * populations[item]
        moment_z = moment_z + velocity_z[item] * populations[item]
    flow_x = (moment_x + 0.5 * field[0]) / density
    flow_y = (moment_y + 0.5 * field[1]) / density
    flow_z = (moment_z + 0.5 * field[2]) / density
    speed_sq = flow_x * flow_x + flow_y * flow_y + flow_z * flow_z
    result = {}
    for item in items:
        ex, ey, ez = (velocity_x[item], velocity_y[item], velocity_z[item])
        weight = lattice_weights[item]
        along = ex * flow_x + ey * flow_y + ez * flow_z
        equilibrium = weight * density * (1.0 + 3.0 * along + 4.5 * along * along - 1.5 * speed_sq)
        push = (ex - flow_x) * field[0] + (ey - flow_y) * field[1] + (ez - flow_z) * field[2]
        facing = ex * field[0] + ey * field[1] + ez * field[2]
        source = weight * (3.0 * push + 9.0 * along * facing)
        current = populations[item]
        result[item] = (
            current - (current - equilibrium) / relax_time + (1.0 - 0.5 / relax_time) * source
        )
    return result


def one_step(displacement, tension, bending, offset, owner, cell, populations):
    membrane_force = membrane(displacement, tension, bending)
    device_count = lax.axis_size("ves") * lax.axis_size("shard")
    slab, width = (populations.shape[0], populations.shape[2])
    cells = slab * width * width
    windows = width // WINDOW
    got = dispatched(membrane_force, offset, owner, cell, device_count, cells)
    tag = got[6].astype(jnp.int32)
    plane, x, y = (tag // (width * width), tag // width % width, tag % width)
    x_bit = bits(slab) + bits(width)
    key = jnp.where(tag >= cells, width << x_bit, (x << x_bit) | (plane << bits(width)) | y)
    bounds = jnp.arange(windows + 1, dtype=jnp.int32) * (WINDOW << x_bit)
    starts = jnp.sum((key[None, :] < bounds[:, None]).astype(jnp.float32), 1)
    ordered = lax.sort(
        (key,) + tuple(got[i] for i in range(6)), num_keys=1, is_stable=False
    )
    listed = jnp.stack(
        list(ordered[1:])
        + [ordered[0].astype(jnp.float32), jnp.pad(starts, (0, key.size - windows - 1))],
        0,
    )
    below = passed_along(listed, ("ves", "shard"), 1)
    above = passed_along(listed, ("ves", "shard"), -1)
    total = spread_own(listed, slab, width)

    early = windows // 2
    edge = early * WINDOW - 8
    low_parts, high_parts = ([], [])
    pieces = [
        ([(windows - 1, windows), (0, early)], 0, edge),
        ([(early, windows - 1)], edge, width),
    ]
    for ranges, begin, end in pieces:
        total, field = spread_rest(total, below, above, slab, ranges, end)
        field = field.reshape(slab, 3, end, width)
        top = collide(
            populations[slab - 1, :, begin:end], field[slab - 1, :, begin:end], range(0, 5)
        )
        bottom = collide(populations[0, :, begin:end], field[0, :, begin:end], range(5, 10))
        low = jnp.stack([top[i] for i in range(0, 5)], 0)
        high = jnp.stack([bottom[i] for i in range(5, 10)], 0)
        low_parts.append(passed_along(low, ("ves", "shard"), 1))
        high_parts.append(passed_along(high, ("ves", "shard"), -1))
    force_field = field
    gated, low, high = lax.optimization_barrier((force_field, low, high))
    low_part = jnp.concatenate(low_parts, 1)
    high_part = jnp.concatenate(high_parts, 1)
    planes = []
    for p in range(slab):
        items = [i for i in range(19) if 0 <= p + velocity_z[i] < slab]
        planes.append(collide(populations[p], gated[p], items))
    new_planes = []
    for p in range(slab):
        moved = []
        for i in range(19):
            source = p - velocity_z[i]
            if source < 0:
                value = low_part[i]
            elif source >= slab:
                value = high_part[i - 5]
            else:
                value = planes[source][i]
            moved.append(jnp.roll(value, (velocity_x[i], velocity_y[i]), (0, 1)))
        new_planes.append(jnp.stack(moved, 0))
    return (membrane_force, force_field, jnp.stack(new_planes, 0))


def solution(mesh):
    return jax.shard_map(
        one_step,
        mesh=mesh,
        in_specs=(
            P(None, "ves", "shard", None),
            P("ves"),
            P("ves"),
            P(None, "ves", "shard", None),
            P("ves", "shard", None),
            P("ves", "shard", None),
            P(("ves", "shard"), None, None, None),
        ),
        out_specs=(
            P(None, "ves", "shard", None),
            P(("ves", "shard"), None, None, None),
            P(("ves", "shard"), None, None, None),
        ),
        check_vma=False,
    )
```

```python
import math

import jax
import jax.numpy as jnp
from jax import lax
from jax.experimental import pallas as pl
from jax.experimental.pallas import tpu as pltpu
from jax.sharding import PartitionSpec as P


relax_time = 0.8
velocity_x = [0, 1, -1, 0, 0, 0, 1, -1, 0, 0, 0, 1, -1, 0, 0, 1, 1, -1, -1]
velocity_y = [0, 0, 0, 1, -1, 0, 0, 0, 1, -1, 0, 0, 0, 1, -1, 1, -1, 1, -1]
velocity_z = [1, 1, 1, 1, 1, -1, -1, -1, -1, -1, 0, 0, 0, 0, 0, 0, 0, 0, 0]
lattice_weights = [
    1.0 / 18,
    1.0 / 36,
    1.0 / 36,
    1.0 / 36,
    1.0 / 36,
    1.0 / 18,
    1.0 / 36,
    1.0 / 36,
    1.0 / 36,
    1.0 / 36,
    1.0 / 3,
    1.0 / 18,
    1.0 / 18,
    1.0 / 18,
    1.0 / 18,
    1.0 / 36,
    1.0 / 36,
    1.0 / 36,
    1.0 / 36,
]


def passed_along(value, axis, steps):
    count = lax.axis_size(axis)
    pairs = [(source, (source + steps) % count) for source in range(count)]
    return lax.ppermute(value, axis, pairs)


def with_halo(x, axis, dim, width):
    devices, length = (lax.axis_size(axis), x.shape[dim])
    up = [(i, i + 1) for i in range(devices - 1)]
    down = [(j, i) for i, j in up]
    last = lax.slice_in_dim(x, length - width, length, axis=dim)
    initial = lax.slice_in_dim(x, 0, width, axis=dim)
    before = lax.ppermute(last, axis, up)
    after = lax.ppermute(initial, axis, down)
    return jnp.concatenate([before, x, after], axis=dim)


def laplacian(padded):
    center = padded[:, :, 1:-1]
    return (
        padded[:, :, 2:]
        + padded[:, :, :-2]
        + jnp.roll(center, 1, 3)
        + jnp.roll(center, -1, 3)
        - 4.0 * center
    )


def membrane(displacement, tension, bending):
    padded = with_halo(displacement, "shard", 2, 2)
    wide_first = laplacian(padded)
    rows = wide_first.shape[2]
    place = lax.broadcasted_iota(jnp.int32, (1, 1, rows, 1), 2)
    index = lax.axis_index("shard")
    outside = ((place == 0) & (index == 0)) | (
        (place == rows - 1) & (index == lax.axis_size("shard") - 1)
    )
    wide_first = jnp.where(outside, 0.0, wide_first)
    second = laplacian(wide_first)
    first = wide_first[:, :, 1:-1]
    return tension[None, :, None, None] * first - bending[None, :, None, None] * second


WINDOW = 16
ROWS = 24
BLOCK = 256


HALF_PI = 0.5 * math.pi
COSINE = [(-1.0) ** n * HALF_PI ** (2 * n) / math.factorial(2 * n) for n in range(8)]
SINE = [(-1.0) ** n * HALF_PI ** (2 * n + 1) / math.factorial(2 * n + 1) for n in range(8)]


def weights(fraction):
    square = fraction * fraction
    c = jnp.full_like(square, COSINE[-1])
    s = jnp.full_like(square, SINE[-1])
    for n in range(6, -1, -1):
        c = c * square + COSINE[n]
        s = s * square + SINE[n]
    s = s * fraction
    return [0.25 * (1.0 - s), 0.25 * (1.0 + c), 0.25 * (1.0 + s), 0.25 * (1.0 - c)]


def bits(count):
    return (count - 1).bit_length()


def spread_list(starts, list_ref, acc, shift, planes, slab, ranges):
    width = acc.shape[2]
    row_id = lax.broadcasted_iota(jnp.int32, (ROWS, BLOCK), 0)
    y_id = lax.broadcasted_iota(jnp.int32, (width, BLOCK), 0)

    def pick(rel, parts):
        result = jnp.zeros(rel.shape, jnp.float32)
        for k in range(4):
            result = jnp.where(rel == k, parts[k], result)
        return result

    def window(w):
        begin = starts[w] // BLOCK
        end = (starts[w + 1] + (BLOCK - 1)) // BLOCK
        base = w * WINDOW

        @pl.loop(begin, end)
        def _(b):
            at = pl.ds(pl.multiple_of(b * BLOCK, BLOCK), BLOCK)
            phi = weights(list_ref[3:6, at])
            key = list_ref[6:7, at].astype(jnp.int32)
            y = key & ((1 << bits(width)) - 1)
            plane = (key >> bits(width)) & ((1 << bits(slab)) - 1)
            x = (key >> (bits(width) + bits(slab))) - base
            x = jnp.where((x >= 0) & (x < WINDOW), x, 4 * ROWS)
            weight_x = pick(row_id - x, [phi[k][0:1] for k in range(4)])
            right = pick((y_id - (y - 1)) & (width - 1), [phi[k][1:2] for k in range(4)])
            lefts = []
            for q in planes:
                weight_z = pick(q + 1 + shift - plane, [phi[k][2:3] for k in range(4)])
                for c in range(3):
                    lefts.append((list_ref[c : c + 1, at] * weight_z) * weight_x)
            product = lax.dot_general(
                jnp.concatenate(lefts, 0).astype(jnp.bfloat16),
                right.astype(jnp.bfloat16),
                (((1,), (1,)), ((), ())),
                preferred_element_type=jnp.float32,
            )
            rows = pl.ds(pl.multiple_of(base, 8), ROWS)
            for n, q in enumerate(planes):
                for c in range(3):
                    i = n * 3 + c
                    acc[q * 3 + c, rows, :] += product[i * ROWS : (i + 1) * ROWS]

    for first, last in ranges:

        @pl.loop(first, last)
        def _(w):
            window(w)


VMEM = pl.BlockSpec(memory_space=pltpu.VMEM)
SMEM = pl.BlockSpec(memory_space=pltpu.SMEM)


def cost(flops):
    return pl.CostEstimate(flops=flops, bytes_accessed=4_000_000, transcendentals=0)


def starts_of(listed, windows):
    return listed[7, : windows + 1].astype(jnp.int32)


def spread_own(listed, slab, width):
    windows = width // WINDOW

    def kernel(starts, list_ref, acc):
        acc[...] = jnp.zeros_like(acc)
        spread_list(starts, list_ref, acc, 0, range(slab), slab, [(0, windows)])

    return pl.pallas_call(
        kernel,
        out_shape=jax.ShapeDtypeStruct((slab * 3, width + ROWS - WINDOW, width), jnp.float32),
        in_specs=[SMEM, VMEM],
        out_specs=VMEM,
        name="spread_own",
        cost_estimate=cost(20_000_000_000),
    )(starts_of(listed, windows), listed)


def spread_rest(total, below, above, slab, ranges, rows):
    width = total.shape[2]
    windows = width // WINDOW

    def kernel(s0, l0, s1, l1, total_ref, acc, out):
        acc[...] = total_ref[...]
        spread_list(s0, l0, acc, slab, (0, 1), slab, ranges)
        spread_list(s1, l1, acc, -slab, (slab - 1,), slab, ranges)
        for i in range(slab * 3):
            out[i] = acc[i, 1 : rows + 1, :]
            out[i, 0:2, :] += acc[i, width + 1 : width + 3, :]
            if rows == width:
                out[i, width - 1 : width, :] += acc[i, 0:1, :]

    return pl.pallas_call(
        kernel,
        out_shape=(
            jax.ShapeDtypeStruct(total.shape, jnp.float32),
            jax.ShapeDtypeStruct((slab * 3, rows, width), jnp.float32),
        ),
        in_specs=[SMEM, VMEM, SMEM, VMEM, VMEM],
        out_specs=(VMEM, VMEM),
        name="spread_rest",
        cost_estimate=cost(15_000_000_000),
    )(starts_of(below, windows), below, starts_of(above, windows), above, total)


def dispatched(membrane_force, offset, owner, cell, device_count, cells):
    point_count = owner.size
    capacity = 2 * point_count // device_count
    slot_total = device_count * capacity
    owner = owner.reshape(point_count)
    cell = cell.reshape(point_count)
    devices = jnp.arange(device_count, dtype=jnp.int32)
    counts = jnp.sum((owner[None, :] == devices[:, None]).astype(jnp.int32), 1)
    filler_ends = jnp.cumsum(capacity - counts)
    filler = jnp.arange(slot_total - point_count, dtype=jnp.int32)
    filler_owner = jnp.sum((filler[None, :] >= filler_ends[:, None]).astype(jnp.int32), 0)
    span = 2 * cells
    key = jnp.concatenate([owner * span + cell, filler_owner * span + cells])
    payload = jnp.concatenate(
        [membrane_force.reshape(3, point_count), offset.reshape(3, point_count)], 0
    )
    payload = jnp.pad(payload, ((0, 0), (0, slot_total - point_count)))
    ordered = lax.sort(
        (key,) + tuple(payload[i] for i in range(6)), num_keys=1, is_stable=False
    )
    tag = (ordered[0] % span).astype(jnp.float32)
    send = jnp.stack(
        [v.reshape(device_count, capacity) for v in list(ordered[1:]) + [tag]], 1
    )
    got = lax.all_to_all(send, ("ves", "shard"), split_axis=0, concat_axis=0, tiled=True)
    return got.transpose(1, 0, 2).reshape(7, slot_total)


def collide(populations, field, items):
    density = jnp.sum(populations, 0)
    moment_x = jnp.zeros_like(density)
    moment_y = jnp.zeros_like(density)
    moment_z = jnp.zeros_like(density)
    for item in range(19):
        moment_x = moment_x + velocity_x[item] * populations[item]
        moment_y = moment_y + velocity_y[item] * populations[item]
        moment_z = moment_z + velocity_z[item] * populations[item]
    flow_x = (moment_x + 0.5 * field[0]) / density
    flow_y = (moment_y + 0.5 * field[1]) / density
    flow_z = (moment_z + 0.5 * field[2]) / density
    speed_sq = flow_x * flow_x + flow_y * flow_y + flow_z * flow_z
    result = {}
    for item in items:
        ex, ey, ez = (velocity_x[item], velocity_y[item], velocity_z[item])
        weight = lattice_weights[item]
        along = ex * flow_x + ey * flow_y + ez * flow_z
        equilibrium = weight * density * (1.0 + 3.0 * along + 4.5 * along * along - 1.5 * speed_sq)
        push = (ex - flow_x) * field[0] + (ey - flow_y) * field[1] + (ez - flow_z) * field[2]
        facing = ex * field[0] + ey * field[1] + ez * field[2]
        source = weight * (3.0 * push + 9.0 * along * facing)
        current = populations[item]
        result[item] = (
            current - (current - equilibrium) / relax_time + (1.0 - 0.5 / relax_time) * source
        )
    return result


def one_step(displacement, tension, bending, offset, owner, cell, populations):
    membrane_force = membrane(displacement, tension, bending)
    device_count = lax.axis_size("ves") * lax.axis_size("shard")
    slab, width = (populations.shape[0], populations.shape[2])
    cells = slab * width * width
    windows = width // WINDOW
    got = dispatched(membrane_force, offset, owner, cell, device_count, cells)
    tag = got[6].astype(jnp.int32)
    plane, x, y = (tag // (width * width), tag // width % width, tag % width)
    x_bit = bits(slab) + bits(width)
    key = jnp.where(tag >= cells, width << x_bit, (x << x_bit) | (plane << bits(width)) | y)
    bounds = jnp.arange(windows + 1, dtype=jnp.int32) * (WINDOW << x_bit)
    starts = jnp.sum((key[None, :] < bounds[:, None]).astype(jnp.float32), 1)
    ordered = lax.sort(
        (key,) + tuple(got[i] for i in range(6)), num_keys=1, is_stable=False
    )
    listed = jnp.stack(
        list(ordered[1:])
        + [ordered[0].astype(jnp.float32), jnp.pad(starts, (0, key.size - windows - 1))],
        0,
    )
    below = passed_along(listed, ("ves", "shard"), 1)
    above = passed_along(listed, ("ves", "shard"), -1)
    total = spread_own(listed, slab, width)

    low_parts, high_parts = ([], [])
    cuts = [windows // 4, windows * 9 // 16]
    edges = [cut * WINDOW - 8 for cut in cuts]
    pieces = [
        ([(windows - 1, windows), (0, cuts[0])], 0, edges[0]),
        ([(cuts[0], cuts[1])], edges[0], edges[1]),
        ([(cuts[1], windows - 1)], edges[1], width),
    ]
    for ranges, begin, end in pieces:
        total, field = spread_rest(total, below, above, slab, ranges, end)
        field = field.reshape(slab, 3, end, width)
        top = collide(
            populations[slab - 1, :, begin:end], field[slab - 1, :, begin:end], range(0, 5)
        )
        bottom = collide(populations[0, :, begin:end], field[0, :, begin:end], range(5, 10))
        low = jnp.stack([top[i] for i in range(0, 5)], 0)
        high = jnp.stack([bottom[i] for i in range(5, 10)], 0)
        low_parts.append(passed_along(low, ("ves", "shard"), 1))
        high_parts.append(passed_along(high, ("ves", "shard"), -1))
    force_field = field
    gated, low, high = lax.optimization_barrier((force_field, low, high))
    low_part = jnp.concatenate(low_parts, 1)
    high_part = jnp.concatenate(high_parts, 1)
    planes = []
    for p in range(slab):
        items = [i for i in range(19) if 0 <= p + velocity_z[i] < slab]
        planes.append(collide(populations[p], gated[p], items))
    new_planes = []
    for p in range(slab):
        moved = []
        for i in range(19):
            source = p - velocity_z[i]
            if source < 0:
                value = low_part[i]
            elif source >= slab:
                value = high_part[i - 5]
            else:
                value = planes[source][i]
            moved.append(jnp.roll(value, (velocity_x[i], velocity_y[i]), (0, 1)))
        new_planes.append(jnp.stack(moved, 0))
    return (membrane_force, force_field, jnp.stack(new_planes, 0))


def solution(mesh):
    return jax.shard_map(
        one_step,
        mesh=mesh,
        in_specs=(
            P(None, "ves", "shard", None),
            P("ves"),
            P("ves"),
            P(None, "ves", "shard", None),
            P("ves", "shard", None),
            P("ves", "shard", None),
            P(("ves", "shard"), None, None, None),
        ),
        out_specs=(
            P(None, "ves", "shard", None),
            P(("ves", "shard"), None, None, None),
            P(("ves", "shard"), None, None, None),
        ),
        check_vma=False,
    )
```
